32 devices in a mesh: row: 4 (over y, core), col: 8 (over z, x).
Axes of the slice: x: 2, y: 2, z: 4, core: 2. Of those that a mesh axis runs over, the one named last changes fastest.
Arguments:
- rhs_tile: float32 [18432, 9216], P('row', 'col'), may hold values from -6 to 6
- factor: float32 [18432, 1536], P('row', 'col'), may hold values from -1 to 2.5, as said below
Outputs:
- whitened: float32 [18432, 9216], P('row', 'col')
The draws below stay inside these ranges and needn't reach their ends.
Inputs may be any that keep to these rules, and one draw needn't show every extreme that they name: In elimination order factor is lower triangular: entries above the diagonal are zero, diagonal entries are at least 0.7.
All inputs are finite; a program needn't handle non-finite values.
Results may differ from the reference program's by a relative error of at most 0.0001.
Values sent between devices are 32-bit elements; how exact they have to be, the bound alone decides.
A program may use at most 128 MiB of HBM per device.

```python
import jax
import jax.numpy as jnp
from jax import lax

N = 18432
PANEL = 512
PANELS = 3
ROWS_DEV = 4608
PB = 128
CB = 64
NRHS = 9216


def draw_factor(key, part):
    window = PANELS * PANEL
    stored = jnp.arange(N).astype(jnp.int32)[:, None]
    column = jnp.arange(window).astype(jnp.int32)[None, :]
    local_row = stored % ROWS_DEV
    stored_panel = local_row // PB
    row_rank = jnp.where(stored_panel < PANELS, stored_panel * PANEL + stored // ROWS_DEV * PB + local_row % PB, window + local_row)
    col_owner = column // (PANELS * CB)
    col_local = column % (PANELS * CB)
    col_panel = col_local // CB
    col_rank = col_panel * PANEL + col_owner * CB + col_local % CB
    key_noise = jax.random.fold_in(key, 11)
    key_diag = jax.random.fold_in(key, 23)
    normal_draw = jnp.clip(jax.random.normal(key_noise, (N, window), jnp.float32), -6.0, 6.0)
    diag_vals = jax.random.uniform(key_diag, (N, window), jnp.float32, 1.0, 2.0)
    near_scale = 0.5
    far_scale = 1.0
    same_panel = row_rank // PANEL == col_panel
    lower_vals = jnp.where(same_panel, normal_draw * (near_scale / jnp.sqrt(1.0 * PANEL)), normal_draw * (far_scale / jnp.sqrt(1.0 * window)))
    values = jnp.where(row_rank == col_rank, diag_vals, jnp.where(row_rank > col_rank, lower_vals, 0.0))
    return values.astype(jnp.float32)


def shard_levels(rng, extent, pieces, smallest, largest):
    def one(dim, blocks):
        steps = jax.random.uniform(jax.random.fold_in(jax.random.fold_in(rng, 6), dim), (blocks,), jnp.float32, smallest / len(pieces), largest / len(pieces))
        return jnp.repeat(jnp.exp(steps), extent[dim] // blocks).reshape((-1,) + (1,) * (len(extent) - dim - 1))

    level = one(*pieces[0])
    for cut in pieces[1:]:
        level = level * one(*cut)
    return level


def bell_draw(key, dims, deviation, limit, shards=(), kind=jnp.bfloat16):
    values = deviation * jax.random.normal(key, dims, jnp.float32)
    if shards:
        values = values * shard_levels(key, dims, shards, -0.22, 0.18)
    return jnp.clip(values, -limit, limit).astype(kind)


def setup_inputs(seed: int = 0) -> dict:
    key_of = jax.random.split(jax.random.key(seed), 3)
    rhs_tile = bell_draw(key_of[0], (N, NRHS), 1.0, 6.0, ((0, 4), (1, 8)), jnp.float32)
    factor = draw_factor(jax.random.fold_in(key_of[2], 71), 0)
    return {"rhs_tile": rhs_tile, "factor": factor}


def reference(rhs_tile, factor):
    window = PANELS * PANEL
    index_k = jnp.arange(window).astype(jnp.int32)
    panel_of = index_k // PANEL
    within = index_k % PANEL
    rows_index = (within // PB * ROWS_DEV + panel_of * PB + within % PB).astype(jnp.int32)
    cols_index = (within // CB * (PANELS * CB) + panel_of * CB + within % CB).astype(jnp.int32)
    factor_cols = factor[:, cols_index]
    stored = jnp.arange(N).astype(jnp.int32)
    local_row = stored % ROWS_DEV
    stored_panel = local_row // PB
    order_rank = jnp.where(stored_panel < PANELS, stored_panel * PANEL + stored // ROWS_DEV * PB + local_row % PB, window)
    result = rhs_tile
    for panel_index in range(PANELS):
        start_row = panel_index * PANEL
        end_row = start_row + PANEL
        panel_rows = rows_index[start_row:end_row]
        diagonal = factor_cols[panel_rows][:, start_row:end_row]
        solved = jax.scipy.linalg.solve_triangular(diagonal, result[panel_rows], lower=True)
        update = jnp.dot(factor_cols[:, start_row:end_row].astype(jnp.float32), solved.astype(jnp.float32), precision=lax.Precision.HIGHEST, preferred_element_type=jnp.float32)
        result = jnp.where((order_rank >= end_row)[:, None], result - update, result)
        result = result.at[panel_rows].set(solved)
    return result
```

```python
import functools

import jax
import jax.numpy as jnp
from jax import lax
from jax.experimental import pallas as pl
from jax.experimental.pallas import tpu as pltpu
from jax.sharding import PartitionSpec as P

PANEL = 512
PANELS = 3
HIGHEST = lax.Precision.HIGHEST
MESH = pl.DeviceIdType.MESH
BF16 = jnp.bfloat16


def exact(x, y):
    return jnp.dot(x, y, precision=HIGHEST, preferred_element_type=jnp.float32)


def split(x):
    high = x.astype(BF16)
    return high, (x - high.astype(jnp.float32)).astype(BF16)


def product(a_high, a_low, b_high, b_low):
    dot = functools.partial(jnp.dot, preferred_element_type=jnp.float32)
    return dot(a_high, b_low) + dot(a_low, b_high) + dot(a_high, b_high)


def invert_triangular(blocks):
    size = blocks[0].shape[-1]
    r = lax.broadcasted_iota(jnp.int32, (size, size), 0)
    c = lax.broadcasted_iota(jnp.int32, (size, size), 1)
    inverses = [jnp.where(r == c, 1.0 / jnp.where(r == c, b, 1.0), 0.0) for b in blocks]
    shift = 0
    while (1 << shift) < size:
        off = ((r >> (shift + 1)) == (c >> (shift + 1))) & ((r >> shift) != (c >> shift))
        inner = [exact(i, jnp.where(off, b, 0.0)) for i, b in zip(inverses, blocks)]
        inverses = [i - exact(m, i) for i, m in zip(inverses, inner)]
        shift += 1
    return inverses


def kernel(
    outer, inner, peers,
    rhs_ref, own_ref, out_ref,
    full_ref, x_ref, lt_ref, inv_ref, high_ref, low_ref, rb_ref, ah_ref, al_ref,
    first_send, first_recv, send_sem, recv_sem, stay_sem, xsend, xrecv, xstay, lsend, lrecv, isend, irecv,
    rload, rstore, ostore,
):
    row = lax.axis_index("row")
    col = lax.axis_index("col")
    a, b = lax.div(col, inner), lax.rem(col, inner)
    blocks = outer * inner
    half = peers // 2
    rp = PANEL // peers
    window = PANELS * rp
    wide = lt_ref.shape[-1]
    tiles = own_ref.shape[-1] // wide
    piece = PANEL // blocks
    columns = rhs_ref.shape[1]
    k, y = lax.rem(row, 2), lax.div(row, 2)
    partner = row + 1 - 2 * k
    far = [lax.rem(y + m, half) * 2 + k for m in range(1, half)]
    far_partner = [lax.rem(y + m, half) * 2 + 1 - k for m in range(1, half)]
    sides = ((1, 0), (-1, 0), (0, 1), (0, -1))
    den = 2 * (outer - 1) * (inner - 1)
    num = min(max(outer * (inner - 1) - (outer - 1), 0), den)

    def inside(da, db):
        return (a + da >= 0) & (a + da < outer) & (b + db >= 0) & (b + db < inner)

    def place(da, db):
        return (a + da) * inner + b + db

    barrier = pltpu.get_barrier_semaphore()
    for da, db in sides:

        @pl.when(inside(da, db))
        def _(da=da, db=db):
            pl.semaphore_signal(barrier, inc=1, device_id=(row, place(da, db)), device_id_type=MESH)

    for m in range(1, peers):
        pl.semaphore_signal(
            barrier, inc=1, device_id=(lax.rem(row + m, peers), col), device_id_type=MESH
        )
    near = sum(inside(da, db).astype(jnp.int32) for da, db in sides)
    pl.semaphore_wait(barrier, near + peers - 1)

    def late(t, origin):
        if den == 0:
            return jnp.bool_(False)
        return lax.rem(t * num + origin * (den // (outer - 1)) + 3, den) < num

    def lanes(t):
        return pl.ds(pl.multiple_of(t * wide, wide), wide)

    def buffer(block, t):
        return full_ref.at[t - 1, :, block]

    def copy(source, block, t, side):
        da, db = sides[side]
        return pltpu.make_async_remote_copy(
            src_ref=source,
            dst_ref=buffer(block, t),
            send_sem=send_sem.at[side, block, t],
            recv_sem=recv_sem.at[block, t],
            device_id=(row, place(da, db)),
            device_id_type=MESH,
        )

    def targets(da, db, t):
        lt = late(t, a + da)
        early = jnp.logical_not(lt)
        chosen = []
        for side, (sa, sb) in enumerate(sides):
            use = inside(sa, sb)
            if (da, db) == (0, 0):
                pass
            elif sa != 0:
                if da * sa > 0:
                    continue
                if da == 0 or db != 0:
                    use = use & lt
            else:
                if db * sb > 0:
                    continue
                if db == 0 or da != 0:
                    use = use & early
            chosen.append((side, use))
        return chosen

    def below(p):
        start = p * rp // 128 * 128
        return pl.ds(start, wide - start)

    def first_copy(block, p, side, own):
        da, db = sides[side]
        here = lt_ref.at[row, p, block, :, below(p)]
        return pltpu.make_async_remote_copy(
            src_ref=own_ref.at[p, :, below(p)] if own else here,
            dst_ref=here,
            send_sem=first_send.at[side, block, p],
            recv_sem=first_recv.at[block, p],
            device_id=(row, place(da, db)),
            device_id_type=MESH,
        )

    def first_launch():
        for side, use in targets(0, 0, 0):

            @pl.when(use)
            def _(side=side):
                for p in range(PANELS):
                    first_copy(col, p, side, True).start()

    def first_pass(ring):
        for da, db in ring:

            @pl.when(inside(da, db))
            def _(da=da, db=db):
                block = place(da, db)
                for p in range(PANELS):
                    first_copy(block, p, 0, False).wait_recv()
                for side, use in targets(da, db, 0):

                    @pl.when(use)
                    def _(side=side):
                        for p in range(PANELS):
                            first_copy(block, p, side, False).start()

    def first_end():
        for da, db in [(0, 0)] + offsets:

            @pl.when(inside(da, db))
            def _(da=da, db=db):
                for side, use in targets(da, db, 0):

                    @pl.when(use)
                    def _(side=side):
                        for p in range(PANELS):
                            first_copy(place(da, db), p, side, False).wait_send()

    def launch(t):
        for side, use in targets(0, 0, t):

            @pl.when(use)
            def _(side=side):
                copy(own_ref.at[:, :, lanes(t)], col, t, side).start()

    offsets = sorted(
        (
            (da, db)
            for da in range(1 - outer, outer)
            for db in range(1 - inner, inner)
            if (da, db) != (0, 0)
        ),
        key=lambda o: (abs(o[0]) + abs(o[1]), o),
    )
    reach = outer + inner - 2
    rings = [[o for o in offsets if abs(o[0]) + abs(o[1]) == d] for d in range(1, reach + 1)]

    def pass_on(t, ring):
        for da, db in ring:

            @pl.when(inside(da, db))
            def _(da=da, db=db):
                block = place(da, db)
                landed = buffer(block, t)
                copy(landed, block, t, 0).wait_recv()
                for side, use in targets(da, db, t):

                    @pl.when(use)
                    def _(side=side):
                        copy(landed, block, t, side).start()

    def x_copy(owner, target, j):
        mine = owner is row
        return pltpu.make_async_remote_copy(
            src_ref=rhs_ref.at[pl.ds(0, window)] if mine else x_ref.at[owner],
            dst_ref=x_ref.at[owner],
            send_sem=xsend.at[j],
            recv_sem=xrecv.at[owner],
            device_id=(target, col),
            device_id_type=MESH,
        )

    def l_copy(p, owner, target, j):
        here = lt_ref.at[owner, p, :, :, below(p)]
        return pltpu.make_async_remote_copy(
            src_ref=here,
            dst_ref=here,
            send_sem=lsend.at[j, p],
            recv_sem=lrecv.at[owner, p],
            device_id=(target, col),
            device_id_type=MESH,
        )

    l_copies = [functools.partial(l_copy, p) for p in range(PANELS)]

    def i_copy(owner, m):
        return pltpu.make_async_remote_copy(
            src_ref=inv_ref.at[owner],
            dst_ref=inv_ref.at[owner],
            send_sem=isend.at[m],
            recv_sem=irecv.at[owner],
            device_id=(lax.rem(row + m, peers), col),
            device_id_type=MESH,
        )

    def share(make):
        for m, target in enumerate(far):
            make(row, target, m + 1).start()
        make(row, partner, 0).start()

    def share_on(make):
        for m, owner in enumerate(far):
            make(owner, partner, half + m).wait_recv()
            make(owner, partner, half + m).start()

    def share_end(make):
        make(partner, partner, 0).wait_recv()
        for m, owner in enumerate(far_partner):
            make(owner, partner, half + m).wait_recv()
        make(row, partner, 0).wait_send()
        for m, target in enumerate(far):
            make(row, target, m + 1).wait_send()
            make(target, partner, half + m).wait_send()

    def invert_own():
        count = rp // piece
        found = []
        for p in range(PANELS):
            block = lt_ref[row, p, pl.ds(row * count, count), :, p * rp : (p + 1) * rp]
            found.append(block.reshape(rp, rp))
        for p, inverse in enumerate(invert_triangular(found)):
            inv_ref[row, p] = inverse.T

    part = columns

    def chunk(n):
        return pl.ds(pl.multiple_of(n * part, part), part)

    def solve(p):
        deep = (p + 1) * PANEL
        here = slice(p * rp, (p + 1) * rp)

        @pl.loop(0, peers)
        def _(r):
            strip = lt_ref[r, : p + 1, :, :, here].reshape(deep, rp).T
            at = pl.ds(pl.multiple_of(r * rp, rp), rp)
            ah_ref[at, :deep], al_ref[at, :deep] = split(strip)

        if p > 0:
            before = p * PANEL

            @pl.loop(0, columns // part)
            def _(n):
                at = chunk(n)
                total = product(
                    ah_ref[:PANEL, :before], al_ref[:PANEL, :before],
                    high_ref[:before, at], low_ref[:before, at],
                )
                for r in range(peers):
                    x_ref[r, here, at] = x_ref[r, here, at] - total[r * rp : (r + 1) * rp]

        for r in range(peers):
            first = p * PANEL
            mine = first + r * rp
            rest = x_ref[r, here, :]
            if r > 0:
                at = slice(r * rp, (r + 1) * rp)
                rest = rest - product(
                    ah_ref[at, first:mine], al_ref[at, first:mine],
                    high_ref[first:mine, :], low_ref[first:mine, :],
                )
            found = product(*split(inv_ref[r, p]), *split(rest))
            x_ref[r, here, :] = found
            high_ref[mine : mine + rp, :], low_ref[mine : mine + rp, :] = split(found)

    def rows(u):
        return pl.ds(pl.multiple_of(u * window, window), window)

    def rhs_load(u):
        slot = lax.rem(u, 2)
        return pltpu.make_async_copy(rhs_ref.at[rows(u)], rb_ref.at[slot], rload.at[slot])

    def store(u):
        slot = lax.rem(u, 2)
        return pltpu.make_async_copy(rb_ref.at[slot], out_ref.at[rows(u)], rstore.at[slot])

    def update(u):
        slot = lax.rem(u, 2)

        @pl.loop(0, PANELS)
        def _(p):
            at = pl.ds(pl.multiple_of(p * PANEL, PANEL), PANEL)
            tile = full_ref[u - 1, p].reshape(PANEL, wide).T
            ah_ref[:wide, at], al_ref[:wide, at] = split(tile)

        rhs_load(u).wait()

        @pl.when(u > 1)
        def _():
            store(u - 1).wait()

        @pl.when(u + 1 < tiles)
        def _():
            rhs_load(u + 1).start()

        @pl.loop(0, columns // part)
        def _(n):
            at = chunk(n)
            total = product(
                ah_ref[:window, :], al_ref[:window, :], high_ref[:, at], low_ref[:, at]
            )
            rb_ref[slot, :, at] = rb_ref[slot, :, at] - total

        store(u).start()

    def keep(t):
        first = isinstance(t, int)
        here = lt_ref.at[row, :, col] if first else buffer(col, t)
        return pltpu.make_async_copy(own_ref.at[:, :, lanes(t)], here, stay_sem.at[t])

    x_stay = pltpu.make_async_copy(rhs_ref.at[pl.ds(0, window)], x_ref.at[row], xstay)

    lead = min(3, tiles)
    ahead = min(6, tiles)
    first_launch()
    keep(0).start()

    @pl.loop(1, tiles)
    def _(t):
        keep(t).start()

    share(x_copy)
    x_stay.start()
    pl.loop(1, lead)(launch)
    for ring in rings:
        first_pass(ring)
    keep(0).wait()

    @pl.loop(1, tiles)
    def _(t):
        keep(t).wait()

    for make in l_copies:
        share(make)
    pl.loop(lead, ahead)(launch)
    rhs_load(1).start()
    invert_own()
    for m in range(1, peers):
        i_copy(row, m).start()
    share_on(x_copy)

    begin = 0
    catch = begin + PANELS
    rate = -(-(tiles - 1) // (tiles - catch))
    lags = [len(rings) - 1 - d for d in range(len(rings))]
    start = 1 - max(lags)

    @pl.loop(start, tiles)
    def _(s):
        @pl.when(s + ahead - start < tiles)
        def _():
            launch(s + ahead - start)

        for lag, ring in zip(lags, rings):
            t = s + lag

            @pl.when((t >= 1) & (t < tiles))
            def _(t=t, ring=ring):
                pass_on(t, ring)

        @pl.when(s == begin)
        def _():
            for make in l_copies:
                share_on(make)
            share_end(x_copy)
            x_stay.wait()
            for make in l_copies:
                share_end(make)
            for m in range(1, peers):
                i_copy(row, m).wait_send()
                i_copy(lax.rem(row + peers - m, peers), m).wait_recv()

        for p in range(PANELS):

            @pl.when(s == begin + p)
            def _(p=p):
                solve(p)

        @pl.when(s >= catch)
        def _():
            low = jnp.minimum(rate * (s - catch) + 1, s)
            high = jnp.minimum(rate * (s - catch) + rate, s)

            @pl.loop(low, high + 1)
            def _(u):
                update(u)

    solved = pltpu.make_async_copy(x_ref.at[row], out_ref.at[pl.ds(0, window)], ostore)
    solved.start()

    first_end()

    @pl.loop(1, tiles)
    def _(t):
        for side, use in targets(0, 0, t):

            @pl.when(use)
            def _(side=side):
                copy(own_ref.at[:, :, lanes(t)], col, t, side).wait_send()

        for da, db in offsets:

            @pl.when(inside(da, db))
            def _(da=da, db=db):
                block = place(da, db)
                for side, use in targets(da, db, t):

                    @pl.when(use)
                    def _(side=side):
                        copy(own_ref.at[:, :, lanes(t)], block, t, side).wait_send()

    store(tiles - 1).wait()
    solved.wait()


def whiten(rhs, own, outer, inner, peers):
    blocks = outer * inner
    window = PANELS * (PANEL // peers)
    tiles = rhs.shape[0] // window
    wide = own.shape[-1] // tiles
    piece = PANEL // blocks
    rp = PANEL // peers
    columns = rhs.shape[1]
    total = PANELS * PANEL
    half = peers // 2
    deepest = max(wide, PANEL)
    dma = pltpu.SemaphoreType.DMA
    any_space = pl.BlockSpec(memory_space=pl.ANY)
    return pl.pallas_call(
        functools.partial(kernel, outer, inner, peers),
        out_shape=jax.ShapeDtypeStruct(rhs.shape, rhs.dtype),
        in_specs=[any_space] * 2,
        out_specs=any_space,
        scratch_shapes=[
            pltpu.VMEM((tiles - 1, PANELS, blocks, piece, wide), jnp.float32),
            pltpu.VMEM((peers, window, columns), jnp.float32),
            pltpu.VMEM((peers, PANELS, blocks, piece, wide), jnp.float32),
            pltpu.VMEM((peers, PANELS, rp, rp), jnp.float32),
            pltpu.VMEM((total, columns), BF16),
            pltpu.VMEM((total, columns), BF16),
            pltpu.VMEM((2, window, columns), jnp.float32),
            pltpu.VMEM((deepest, total), BF16),
            pltpu.VMEM((deepest, total), BF16),
            dma((4, blocks, PANELS)),
            dma((blocks, PANELS)),
            dma((4, blocks, tiles)),
            dma((blocks, tiles)),
            dma((tiles,)),
            dma((2 * half,)),
            dma((peers,)),
            dma,
            dma((2 * half, PANELS)),
            dma((peers, PANELS)),
            dma((peers,)),
            dma((peers,)),
            dma((2,)),
            dma((2,)),
            dma,
        ],
        compiler_params=pltpu.CompilerParams(
            collective_id=0, has_side_effects=True, vmem_limit_bytes=67_043_328
        ),
        cost_estimate=pl.CostEstimate(
            flops=6 * rhs.shape[0] * total * columns,
            bytes_accessed=16 * rhs.size,
            transcendentals=0,
        ),
    )(rhs, own)


def local(rhs_tile, factor, inner):
    peers = lax.axis_size("row")
    blocks = lax.axis_size("col")
    window = PANELS * (PANEL // peers)
    own = factor.T.reshape(PANELS, PANEL // blocks, factor.shape[0])
    if window % 128:
        own = own.reshape(PANELS, PANEL // blocks, -1, window)
        own = jnp.pad(own, ((0, 0), (0, 0), (0, 0), (0, -window % 128)))
        own = own.reshape(PANELS, PANEL // blocks, -1)
    return whiten(rhs_tile, own, blocks // inner, inner, peers)


def inner_size(mesh):
    count = mesh.shape["col"]
    try:
        where = [tuple(d.coords) for d in mesh.devices.reshape(-1, count)[0]]
        inner = 1
        while inner < count and sum(p != q for p, q in zip(where[inner], where[0])) == 1 and (
            inner == 1 or [p != q for p, q in zip(where[inner], where[0])]
            == [p != q for p, q in zip(where[1], where[0])]
        ):
            inner += 1
        if count % inner == 0:
            return inner
    except Exception:
        pass
    return 2 if count % 2 == 0 else 1


def solution(mesh):
    specs = P("row", "col")
    body = functools.partial(local, inner=inner_size(mesh))
    return jax.shard_map(body, mesh=mesh, in_specs=(specs, specs), out_specs=specs, check_vma=False)
```

```python
import functools

import jax
import jax.numpy as jnp
from jax import lax
from jax.experimental import pallas as pl
from jax.experimental.pallas import tpu as pltpu
from jax.sharding import PartitionSpec as P

PANEL = 512
PANELS = 3
HIGHEST = lax.Precision.HIGHEST
MESH = pl.DeviceIdType.MESH
BF16 = jnp.bfloat16


def exact(x, y):
    return jnp.dot(x, y, precision=HIGHEST, preferred_element_type=jnp.float32)


def split(x):
    high = x.astype(BF16)
    return high, (x - high.astype(jnp.float32)).astype(BF16)


def product(a_high, a_low, b_high, b_low):
    dot = functools.partial(jnp.dot, preferred_element_type=jnp.float32)
    return dot(a_high, b_low) + dot(a_low, b_high) + dot(a_high, b_high)


def invert_triangular(blocks):
    size = blocks[0].shape[-1]
    r = lax.broadcasted_iota(jnp.int32, (size, size), 0)
    c = lax.broadcasted_iota(jnp.int32, (size, size), 1)
    inverses = [jnp.where(r == c, 1.0 / jnp.where(r == c, b, 1.0), 0.0) for b in blocks]
    shift = 0
    while (1 << shift) < size:
        off = ((r >> (shift + 1)) == (c >> (shift + 1))) & ((r >> shift) != (c >> shift))
        inner = [exact(i, jnp.where(off, b, 0.0)) for i, b in zip(inverses, blocks)]
        inverses = [i - exact(m, i) for i, m in zip(inverses, inner)]
        shift += 1
    return inverses


def kernel(
    outer, inner, peers,
    rhs_ref, own_ref, out_ref,
    full_ref, x_ref, lt_ref, inv_ref, high_ref, low_ref, rb_ref, ah_ref, al_ref,
    first_send, first_recv, send_sem, recv_sem, stay_sem, xsend, xrecv, xstay, lsend, lrecv, isend, irecv,
    rload, rstore, ostore,
):
    row = lax.axis_index("row")
    col = lax.axis_index("col")
    a, b = lax.div(col, inner), lax.rem(col, inner)
    blocks = outer * inner
    half = peers // 2
    rp = PANEL // peers
    window = PANELS * rp
    wide = lt_ref.shape[-1]
    tiles = own_ref.shape[-1] // wide
    piece = PANEL // blocks
    columns = rhs_ref.shape[1]
    k, y = lax.rem(row, 2), lax.div(row, 2)
    partner = row + 1 - 2 * k
    far = [lax.rem(y + m, half) * 2 + k for m in range(1, half)]
    far_partner = [lax.rem(y + m, half) * 2 + 1 - k for m in range(1, half)]
    sides = ((1, 0), (-1, 0), (0, 1), (0, -1))
    den = 2 * (outer - 1) * (inner - 1)
    num = min(max(outer * (inner - 1) - (outer - 1), 0), den)

    def inside(da, db):
        return (a + da >= 0) & (a + da < outer) & (b + db >= 0) & (b + db < inner)

    def place(da, db):
        return (a + da) * inner + b + db

    barrier = pltpu.get_barrier_semaphore()
    for da, db in sides:

        @pl.when(inside(da, db))
        def _(da=da, db=db):
            pl.semaphore_signal(barrier, inc=1, device_id=(row, place(da, db)), device_id_type=MESH)

    for m in range(1, peers):
        pl.semaphore_signal(
            barrier, inc=1, device_id=(lax.rem(row + m, peers), col), device_id_type=MESH
        )
    near = sum(inside(da, db).astype(jnp.int32) for da, db in sides)
    pl.semaphore_wait(barrier, near + peers - 1)

    def late(t, origin):
        if den == 0:
            return jnp.bool_(False)
        return lax.rem(t * num + origin * (den // (outer - 1)) + 4, den) < num

    def lanes(t):
        return pl.ds(pl.multiple_of(t * wide, wide), wide)

    def buffer(block, t):
        return full_ref.at[t - 1, :, block]

    def copy(source, block, t, side):
        da, db = sides[side]
        return pltpu.make_async_remote_copy(
            src_ref=source,
            dst_ref=buffer(block, t),
            send_sem=send_sem.at[side, block, t],
            recv_sem=recv_sem.at[block, t],
            device_id=(row, place(da, db)),
            device_id_type=MESH,
        )

    def targets(da, db, t):
        lt = late(t, a + da)
        early = jnp.logical_not(lt)
        chosen = []
        for side, (sa, sb) in enumerate(sides):
            use = inside(sa, sb)
            if (da, db) == (0, 0):
                pass
            elif sa != 0:
                if da * sa > 0:
                    continue
                if da == 0 or db != 0:
                    use = use & lt
            else:
                if db * sb > 0:
                    continue
                if db == 0 or da != 0:
                    use = use & early
            chosen.append((side, use))
        return chosen

    def below(p):
        start = p * rp // 128 * 128
        return pl.ds(start, wide - start)

    def first_copy(block, p, side, own):
        da, db = sides[side]
        here = lt_ref.at[row, p, block, :, below(p)]
        return pltpu.make_async_remote_copy(
            src_ref=own_ref.at[p, :, below(p)] if own else here,
            dst_ref=here,
            send_sem=first_send.at[side, block, p],
            recv_sem=first_recv.at[block, p],
            device_id=(row, place(da, db)),
            device_id_type=MESH,
        )

    def first_launch():
        for side, use in targets(0, 0, 0):

            @pl.when(use)
            def _(side=side):
                for p in range(PANELS):
                    first_copy(col, p, side, True).start()

    def first_pass(ring):
        for da, db in ring:

            @pl.when(inside(da, db))
            def _(da=da, db=db):
                block = place(da, db)
                for p in range(PANELS):
                    first_copy(block, p, 0, False).wait_recv()
                for side, use in targets(da, db, 0):

                    @pl.when(use)
                    def _(side=side):
                        for p in range(PANELS):
                            first_copy(block, p, side, False).start()

    def first_end():
        for da, db in [(0, 0)] + offsets:

            @pl.when(inside(da, db))
            def _(da=da, db=db):
                for side, use in targets(da, db, 0):

                    @pl.when(use)
                    def _(side=side):
                        for p in range(PANELS):
                            first_copy(place(da, db), p, side, False).wait_send()

    def launch(t):
        for side, use in targets(0, 0, t):

            @pl.when(use)
            def _(side=side):
                copy(own_ref.at[:, :, lanes(t)], col, t, side).start()

    offsets = sorted(
        (
            (da, db)
            for da in range(1 - outer, outer)
            for db in range(1 - inner, inner)
            if (da, db) != (0, 0)
        ),
        key=lambda o: (abs(o[0]) + abs(o[1]), o),
    )
    reach = outer + inner - 2
    rings = [[o for o in offsets if abs(o[0]) + abs(o[1]) == d] for d in range(1, reach + 1)]

    def pass_on(t, ring):
        for da, db in ring:

            @pl.when(inside(da, db))
            def _(da=da, db=db):
                block = place(da, db)
                landed = buffer(block, t)
                copy(landed, block, t, 0).wait_recv()
                for side, use in targets(da, db, t):

                    @pl.when(use)
                    def _(side=side):
                        copy(landed, block, t, side).start()

    def x_copy(owner, target, j):
        mine = owner is row
        return pltpu.make_async_remote_copy(
            src_ref=rhs_ref.at[pl.ds(0, window)] if mine else x_ref.at[owner],
            dst_ref=x_ref.at[owner],
            send_sem=xsend.at[j],
            recv_sem=xrecv.at[owner],
            device_id=(target, col),
            device_id_type=MESH,
        )

    def l_copy(p, owner, target, j):
        here = lt_ref.at[owner, p, :, :, below(p)]
        return pltpu.make_async_remote_copy(
            src_ref=here,
            dst_ref=here,
            send_sem=lsend.at[j, p],
            recv_sem=lrecv.at[owner, p],
            device_id=(target, col),
            device_id_type=MESH,
        )

    l_copies = [functools.partial(l_copy, p) for p in range(PANELS)]

    def i_copy(owner, m):
        return pltpu.make_async_remote_copy(
            src_ref=inv_ref.at[owner],
            dst_ref=inv_ref.at[owner],
            send_sem=isend.at[m],
            recv_sem=irecv.at[owner],
            device_id=(lax.rem(row + m, peers), col),
            device_id_type=MESH,
        )

    def share(make):
        for m, target in enumerate(far):
            make(row, target, m + 1).start()
        make(row, partner, 0).start()

    def share_on(make):
        for m, owner in enumerate(far):
            make(owner, partner, half + m).wait_recv()
            make(owner, partner, half + m).start()

    def share_end(make):
        make(partner, partner, 0).wait_recv()
        for m, owner in enumerate(far_partner):
            make(owner, partner, half + m).wait_recv()
        make(row, partner, 0).wait_send()
        for m, target in enumerate(far):
            make(row, target, m + 1).wait_send()
            make(target, partner, half + m).wait_send()

    def invert_own():
        count = rp // piece
        found = []
        for p in range(PANELS):
            block = lt_ref[row, p, pl.ds(row * count, count), :, p * rp : (p + 1) * rp]
            found.append(block.reshape(rp, rp))
        for p, inverse in enumerate(invert_triangular(found)):
            inv_ref[row, p] = inverse.T

    part = columns

    def chunk(n):
        return pl.ds(pl.multiple_of(n * part, part), part)

    def solve(p):
        deep = (p + 1) * PANEL
        here = slice(p * rp, (p + 1) * rp)

        @pl.loop(0, peers)
        def _(r):
            strip = lt_ref[r, : p + 1, :, :, here].reshape(deep, rp).T
            at = pl.ds(pl.multiple_of(r * rp, rp), rp)
            ah_ref[at, :deep], al_ref[at, :deep] = split(strip)

        if p > 0:
            before = p * PANEL

            @pl.loop(0, columns // part)
            def _(n):
                at = chunk(n)
                total = product(
                    ah_ref[:PANEL, :before], al_ref[:PANEL, :before],
                    high_ref[:before, at], low_ref[:before, at],
                )
                for r in range(peers):
                    x_ref[r, here, at] = x_ref[r, here, at] - total[r * rp : (r + 1) * rp]

        for r in range(peers):
            first = p * PANEL
            mine = first + r * rp
            rest = x_ref[r, here, :]
            if r > 0:
                at = slice(r * rp, (r + 1) * rp)
                rest = rest - product(
                    ah_ref[at, first:mine], al_ref[at, first:mine],
                    high_ref[first:mine, :], low_ref[first:mine, :],
                )
            found = product(*split(inv_ref[r, p]), *split(rest))
            x_ref[r, here, :] = found
            high_ref[mine : mine + rp, :], low_ref[mine : mine + rp, :] = split(found)

    def rows(u):
        return pl.ds(pl.multiple_of(u * window, window), window)

    def rhs_load(u):
        slot = lax.rem(u, 2)
        return pltpu.make_async_copy(rhs_ref.at[rows(u)], rb_ref.at[slot], rload.at[slot])

    def store(u):
        slot = lax.rem(u, 2)
        return pltpu.make_async_copy(rb_ref.at[slot], out_ref.at[rows(u)], rstore.at[slot])

    def update(u):
        slot = lax.rem(u, 2)

        @pl.loop(0, PANELS)
        def _(p):
            at = pl.ds(pl.multiple_of(p * PANEL, PANEL), PANEL)
            tile = full_ref[u - 1, p].reshape(PANEL, wide).T
            ah_ref[:wide, at], al_ref[:wide, at] = split(tile)

        rhs_load(u).wait()

        @pl.when(u > 1)
        def _():
            store(u - 1).wait()

        @pl.when(u + 1 < tiles)
        def _():
            rhs_load(u + 1).start()

        @pl.loop(0, columns // part)
        def _(n):
            at = chunk(n)
            total = product(
                ah_ref[:window, :], al_ref[:window, :], high_ref[:, at], low_ref[:, at]
            )
            rb_ref[slot, :, at] = rb_ref[slot, :, at] - total

        store(u).start()

    def keep(t):
        first = isinstance(t, int)
        here = lt_ref.at[row, :, col] if first else buffer(col, t)
        return pltpu.make_async_copy(own_ref.at[:, :, lanes(t)], here, stay_sem.at[t])

    x_stay = pltpu.make_async_copy(rhs_ref.at[pl.ds(0, window)], x_ref.at[row], xstay)

    lead = min(3, tiles)
    ahead = min(6, tiles)
    first_launch()
    keep(0).start()

    @pl.loop(1, tiles)
    def _(t):
        keep(t).start()

    share(x_copy)
    x_stay.start()
    pl.loop(1, lead)(launch)
    for ring in rings:
        first_pass(ring)
    keep(0).wait()

    @pl.loop(1, tiles)
    def _(t):
        keep(t).wait()

    for make in l_copies:
        share(make)
    pl.loop(lead, ahead)(launch)
    rhs_load(1).start()
    invert_own()
    for m in range(1, peers):
        i_copy(row, m).start()
    share_on(x_copy)

    begin = 0
    catch = begin + PANELS
    rate = -(-(tiles - 1) // (tiles - catch))
    lags = [len(rings) - 1 - d for d in range(len(rings))]
    start = 1 - max(lags)

    solved = pltpu.make_async_copy(x_ref.at[row], out_ref.at[pl.ds(0, window)], ostore)

    @pl.loop(start, tiles)
    def _(s):
        @pl.when(s + ahead - start < tiles)
        def _():
            launch(s + ahead - start)

        for lag, ring in zip(lags, rings):
            t = s + lag

            @pl.when((t >= 1) & (t < tiles))
            def _(t=t, ring=ring):
                pass_on(t, ring)

        @pl.when(s == begin)
        def _():
            for make in l_copies:
                share_on(make)
            share_end(x_copy)
            x_stay.wait()
            for make in l_copies:
                share_end(make)
            for m in range(1, peers):
                i_copy(row, m).wait_send()
                i_copy(lax.rem(row + peers - m, peers), m).wait_recv()

        for p in range(PANELS):

            @pl.when(s == begin + p)
            def _(p=p):
                solve(p)

        @pl.when(s == catch - 1)
        def _():
            solved.start()

        @pl.when(s >= catch)
        def _():
            low = jnp.minimum(rate * (s - catch) + 1, s)
            high = jnp.minimum(rate * (s - catch) + rate, s)

            @pl.loop(low, high + 1)
            def _(u):
                update(u)

    first_end()

    @pl.loop(1, tiles)
    def _(t):
        for side, use in targets(0, 0, t):

            @pl.when(use)
            def _(side=side):
                copy(own_ref.at[:, :, lanes(t)], col, t, side).wait_send()

        for da, db in offsets:

            @pl.when(inside(da, db))
            def _(da=da, db=db):
                block = place(da, db)
                for side, use in targets(da, db, t):

                    @pl.when(use)
                    def _(side=side):
                        copy(own_ref.at[:, :, lanes(t)], block, t, side).wait_send()

    store(tiles - 1).wait()
    solved.wait()


def whiten(rhs, own, outer, inner, peers):
    blocks = outer * inner
    window = PANELS * (PANEL // peers)
    tiles = rhs.shape[0] // window
    wide = own.shape[-1] // tiles
    piece = PANEL // blocks
    rp = PANEL // peers
    columns = rhs.shape[1]
    total = PANELS * PANEL
    half = peers // 2
    deepest = max(wide, PANEL)
    dma = pltpu.SemaphoreType.DMA
    any_space = pl.BlockSpec(memory_space=pl.ANY)
    return pl.pallas_call(
        functools.partial(kernel, outer, inner, peers),
        out_shape=jax.ShapeDtypeStruct(rhs.shape, rhs.dtype),
        in_specs=[any_space] * 2,
        out_specs=any_space,
        scratch_shapes=[
            pltpu.VMEM((tiles - 1, PANELS, blocks, piece, wide), jnp.float32),
            pltpu.VMEM((peers, window, columns), jnp.float32),
            pltpu.VMEM((peers, PANELS, blocks, piece, wide), jnp.float32),
            pltpu.VMEM((peers, PANELS, rp, rp), jnp.float32),
            pltpu.VMEM((total, columns), BF16),
            pltpu.VMEM((total, columns), BF16),
            pltpu.VMEM((2, window, columns), jnp.float32),
            pltpu.VMEM((deepest, total), BF16),
            pltpu.VMEM((deepest, total), BF16),
            dma((4, blocks, PANELS)),
            dma((blocks, PANELS)),
            dma((4, blocks, tiles)),
            dma((blocks, tiles)),
            dma((tiles,)),
            dma((2 * half,)),
            dma((peers,)),
            dma,
            dma((2 * half, PANELS)),
            dma((peers, PANELS)),
            dma((peers,)),
            dma((peers,)),
            dma((2,)),
            dma((2,)),
            dma,
        ],
        compiler_params=pltpu.CompilerParams(
            collective_id=0, has_side_effects=True, vmem_limit_bytes=67_043_328
        ),
        cost_estimate=pl.CostEstimate(
            flops=6 * rhs.shape[0] * total * columns,
            bytes_accessed=16 * rhs.size,
            transcendentals=0,
        ),
    )(rhs, own)


def local(rhs_tile, factor, inner):
    peers = lax.axis_size("row")
    blocks = lax.axis_size("col")
    window = PANELS * (PANEL // peers)
    own = factor.T.reshape(PANELS, PANEL // blocks, factor.shape[0])
    if window % 128:
        own = own.reshape(PANELS, PANEL // blocks, -1, window)
        own = jnp.pad(own, ((0, 0), (0, 0), (0, 0), (0, -window % 128)))
        own = own.reshape(PANELS, PANEL // blocks, -1)
    return whiten(rhs_tile, own, blocks // inner, inner, peers)


def inner_size(mesh):
    count = mesh.shape["col"]
    try:
        where = [tuple(d.coords) for d in mesh.devices.reshape(-1, count)[0]]
        inner = 1
        while inner < count and sum(p != q for p, q in zip(where[inner], where[0])) == 1 and (
            inner == 1 or [p != q for p, q in zip(where[inner], where[0])]
            == [p != q for p, q in zip(where[1], where[0])]
        ):
            inner += 1
        if count % inner == 0:
            return inner
    except Exception:
        pass
    return 2 if count % 2 == 0 else 1


def solution(mesh):
    specs = P("row", "col")
    body = functools.partial(local, inner=inner_size(mesh))
    return jax.shard_map(body, mesh=mesh, in_specs=(specs, specs), out_specs=specs, check_vma=False)
```

```python
import functools

import jax
import jax.numpy as jnp
from jax import lax
from jax.experimental import pallas as pl
from jax.experimental.pallas import tpu as pltpu
from jax.sharding import PartitionSpec as P

PANEL = 512
PANELS = 3
HIGHEST = lax.Precision.HIGHEST
MESH = pl.DeviceIdType.MESH
BF16 = jnp.bfloat16


def exact(x, y):
    return jnp.dot(x, y, precision=HIGHEST, preferred_element_type=jnp.float32)


def split(x):
    high = x.astype(BF16)
    return high, (x - high.astype(jnp.float32)).astype(BF16)


def product(a_high, a_low, b_high, b_low):
    dot = functools.partial(jnp.dot, preferred_element_type=jnp.float32)
    return dot(a_high, b_low) + dot(a_low, b_high) + dot(a_high, b_high)


def invert_triangular(blocks):
    size = blocks[0].shape[-1]
    r = lax.broadcasted_iota(jnp.int32, (size, size), 0)
    c = lax.broadcasted_iota(jnp.int32, (size, size), 1)
    inverses = [jnp.where(r == c, 1.0 / jnp.where(r == c, b, 1.0), 0.0) for b in blocks]
    shift = 0
    while (1 << shift) < size:
        off = ((r >> (shift + 1)) == (c >> (shift + 1))) & ((r >> shift) != (c >> shift))
        inner = [exact(i, jnp.where(off, b, 0.0)) for i, b in zip(inverses, blocks)]
        inverses = [i - exact(m, i) for i, m in zip(inverses, inner)]
        shift += 1
    return inverses


def kernel(
    outer, inner, peers,
    rhs_ref, own_ref, out_ref,
    full_ref, tail_ref, x_ref, lt_ref, inv_ref, high_ref, low_ref, rb_ref, ah_ref, al_ref,
    first_send, first_recv, send_sem, recv_sem, stay_sem, xsend, xrecv, xstay, lsend, lrecv, isend, irecv,
    rload, rstore, ostore, tail_send, tail_recv, tail_stay, tail_done,
):
    row = lax.axis_index("row")
    col = lax.axis_index("col")
    a, b = lax.div(col, inner), lax.rem(col, inner)
    blocks = outer * inner
    half = peers // 2
    rp = PANEL // peers
    window = PANELS * rp
    wide = lt_ref.shape[-1]
    tiles = own_ref.shape[-1] // wide
    last = tiles - 1
    subs, slim = tail_ref.shape[0], tail_ref.shape[-1]
    thin = window // subs
    piece = PANEL // blocks
    columns = rhs_ref.shape[1]
    k, y = lax.rem(row, 2), lax.div(row, 2)
    partner = row + 1 - 2 * k
    far = [lax.rem(y + m, half) * 2 + k for m in range(1, half)]
    far_partner = [lax.rem(y + m, half) * 2 + 1 - k for m in range(1, half)]
    sides = ((1, 0), (-1, 0), (0, 1), (0, -1))
    den = 2 * (outer - 1) * (inner - 1)
    num = min(max(outer * (inner - 1) - (outer - 1), 0), den)

    def inside(da, db):
        return (a + da >= 0) & (a + da < outer) & (b + db >= 0) & (b + db < inner)

    def place(da, db):
        return (a + da) * inner + b + db

    barrier = pltpu.get_barrier_semaphore()
    for da, db in sides:

        @pl.when(inside(da, db))
        def _(da=da, db=db):
            pl.semaphore_signal(barrier, inc=1, device_id=(row, place(da, db)), device_id_type=MESH)

    for m in range(1, peers):
        pl.semaphore_signal(
            barrier, inc=1, device_id=(lax.rem(row + m, peers), col), device_id_type=MESH
        )
    near = sum(inside(da, db).astype(jnp.int32) for da, db in sides)
    pl.semaphore_wait(barrier, near + peers - 1)

    def late(t, origin):
        if den == 0:
            return jnp.bool_(False)
        return lax.rem(t * num + origin * (den // (outer - 1)) + 4, den) < num

    def lanes(t):
        return pl.ds(pl.multiple_of(t * wide, wide), wide)

    def buffer(block, t):
        return full_ref.at[t - 1, :, block]

    def copy(source, block, t, side):
        da, db = sides[side]
        return pltpu.make_async_remote_copy(
            src_ref=source,
            dst_ref=buffer(block, t),
            send_sem=send_sem.at[side, block, t],
            recv_sem=recv_sem.at[block, t],
            device_id=(row, place(da, db)),
            device_id_type=MESH,
        )

    def targets(da, db, t):
        lt = late(t, a + da)
        early = jnp.logical_not(lt)
        chosen = []
        for side, (sa, sb) in enumerate(sides):
            use = inside(sa, sb)
            if (da, db) == (0, 0):
                pass
            elif sa != 0:
                if da * sa > 0:
                    continue
                if da == 0 or db != 0:
                    use = use & lt
            else:
                if db * sb > 0:
                    continue
                if db == 0 or da != 0:
                    use = use & early
            chosen.append((side, use))
        return chosen

    def below(p):
        start = p * rp // 128 * 128
        return pl.ds(start, wide - start)

    def first_copy(block, p, side, own):
        da, db = sides[side]
        here = lt_ref.at[row, p, block, :, below(p)]
        return pltpu.make_async_remote_copy(
            src_ref=own_ref.at[p, :, below(p)] if own else here,
            dst_ref=here,
            send_sem=first_send.at[side, block, p],
            recv_sem=first_recv.at[block, p],
            device_id=(row, place(da, db)),
            device_id_type=MESH,
        )

    def first_launch():
        for side, use in targets(0, 0, 0):

            @pl.when(use)
            def _(side=side):
                for p in range(PANELS):
                    first_copy(col, p, side, True).start()

    def first_pass(ring):
        for da, db in ring:

            @pl.when(inside(da, db))
            def _(da=da, db=db):
                block = place(da, db)
                for p in range(PANELS):
                    first_copy(block, p, 0, False).wait_recv()
                for side, use in targets(da, db, 0):

                    @pl.when(use)
                    def _(side=side):
                        for p in range(PANELS):
                            first_copy(block, p, side, False).start()

    def first_end():
        for da, db in [(0, 0)] + offsets:

            @pl.when(inside(da, db))
            def _(da=da, db=db):
                for side, use in targets(da, db, 0):

                    @pl.when(use)
                    def _(side=side):
                        for p in range(PANELS):
                            first_copy(place(da, db), p, side, False).wait_send()

    def tail_source(j):
        return own_ref.at[:, :, pl.ds(pl.multiple_of(last * wide + j * slim, slim), slim)]

    def tail_copy(source, block, j, side):
        da, db = sides[side]
        return pltpu.make_async_remote_copy(
            src_ref=source,
            dst_ref=tail_ref.at[j, :, block],
            send_sem=tail_send.at[side, block, j],
            recv_sem=tail_recv.at[block, j],
            device_id=(row, place(da, db)),
            device_id_type=MESH,
        )

    def tail_launch(j):
        for side, use in targets(0, 0, last):

            @pl.when(use)
            def _(side=side):
                tail_copy(tail_source(j), col, j, side).start()

    def tail_pass(j, ring):
        for da, db in ring:

            @pl.when(inside(da, db))
            def _(da=da, db=db):
                block = place(da, db)
                landed = tail_ref.at[j, :, block]
                tail_copy(landed, block, j, 0).wait_recv()
                for side, use in targets(da, db, last):

                    @pl.when(use)
                    def _(side=side):
                        tail_copy(landed, block, j, side).start()

    def tail_end(j):
        for da, db in [(0, 0)] + offsets:

            @pl.when(inside(da, db))
            def _(da=da, db=db):
                block = place(da, db)
                for side, use in targets(da, db, last):

                    @pl.when(use)
                    def _(side=side):
                        tail_copy(tail_ref.at[j, :, block], block, j, side).wait_send()

    def tail_keep(j):
        return pltpu.make_async_copy(tail_source(j), tail_ref.at[j, :, col], tail_stay.at[j])

    def launch(t):
        for side, use in targets(0, 0, t):

            @pl.when(use)
            def _(side=side):
                copy(own_ref.at[:, :, lanes(t)], col, t, side).start()

    offsets = sorted(
        (
            (da, db)
            for da in range(1 - outer, outer)
            for db in range(1 - inner, inner)
            if (da, db) != (0, 0)
        ),
        key=lambda o: (abs(o[0]) + abs(o[1]), o),
    )
    reach = outer + inner - 2
    rings = [[o for o in offsets if abs(o[0]) + abs(o[1]) == d] for d in range(1, reach + 1)]

    def pass_on(t, ring):
        for da, db in ring:

            @pl.when(inside(da, db))
            def _(da=da, db=db):
                block = place(da, db)
                landed = buffer(block, t)
                copy(landed, block, t, 0).wait_recv()
                for side, use in targets(da, db, t):

                    @pl.when(use)
                    def _(side=side):
                        copy(landed, block, t, side).start()

    def x_copy(owner, target, j):
        mine = owner is row
        return pltpu.make_async_remote_copy(
            src_ref=rhs_ref.at[pl.ds(0, window)] if mine else x_ref.at[owner],
            dst_ref=x_ref.at[owner],
            send_sem=xsend.at[j],
            recv_sem=xrecv.at[owner],
            device_id=(target, col),
            device_id_type=MESH,
        )

    def l_copy(p, owner, target, j):
        here = lt_ref.at[owner, p, :, :, below(p)]
        return pltpu.make_async_remote_copy(
            src_ref=here,
            dst_ref=here,
            send_sem=lsend.at[j, p],
            recv_sem=lrecv.at[owner, p],
            device_id=(target, col),
            device_id_type=MESH,
        )

    l_copies = [functools.partial(l_copy, p) for p in range(PANELS)]

    def i_copy(owner, m):
        return pltpu.make_async_remote_copy(
            src_ref=inv_ref.at[owner],
            dst_ref=inv_ref.at[owner],
            send_sem=isend.at[m],
            recv_sem=irecv.at[owner],
            device_id=(lax.rem(row + m, peers), col),
            device_id_type=MESH,
        )

    def share(make):
        for m, target in enumerate(far):
            make(row, target, m + 1).start()
        make(row, partner, 0).start()

    def share_on(make):
        for m, owner in enumerate(far):
            make(owner, partner, half + m).wait_recv()
            make(owner, partner, half + m).start()

    def share_end(make):
        make(partner, partner, 0).wait_recv()
        for m, owner in enumerate(far_partner):
            make(owner, partner, half + m).wait_recv()
        make(row, partner, 0).wait_send()
        for m, target in enumerate(far):
            make(row, target, m + 1).wait_send()
            make(target, partner, half + m).wait_send()

    def invert_own():
        count = rp // piece
        found = []
        for p in range(PANELS):
            block = lt_ref[row, p, pl.ds(row * count, count), :, p * rp : (p + 1) * rp]
            found.append(block.reshape(rp, rp))
        for p, inverse in enumerate(invert_triangular(found)):
            inv_ref[row, p] = inverse.T

    part = columns

    def chunk(n):
        return pl.ds(pl.multiple_of(n * part, part), part)

    def solve(p):
        deep = (p + 1) * PANEL
        here = slice(p * rp, (p + 1) * rp)

        @pl.loop(0, peers)
        def _(r):
            strip = lt_ref[r, : p + 1, :, :, here].reshape(deep, rp).T
            at = pl.ds(pl.multiple_of(r * rp, rp), rp)
            ah_ref[at, :deep], al_ref[at, :deep] = split(strip)

        if p > 0:
            before = p * PANEL

            @pl.loop(0, columns // part)
            def _(n):
                at = chunk(n)
                total = product(
                    ah_ref[:PANEL, :before], al_ref[:PANEL, :before],
                    high_ref[:before, at], low_ref[:before, at],
                )
                for r in range(peers):
                    x_ref[r, here, at] = x_ref[r, here, at] - total[r * rp : (r + 1) * rp]

        for r in range(peers):
            first = p * PANEL
            mine = first + r * rp
            rest = x_ref[r, here, :]
            if r > 0:
                at = slice(r * rp, (r + 1) * rp)
                rest = rest - product(
                    ah_ref[at, first:mine], al_ref[at, first:mine],
                    high_ref[first:mine, :], low_ref[first:mine, :],
                )
            found = product(*split(inv_ref[r, p]), *split(rest))
            x_ref[r, here, :] = found
            high_ref[mine : mine + rp, :], low_ref[mine : mine + rp, :] = split(found)

    def rows(u):
        return pl.ds(pl.multiple_of(u * window, window), window)

    def rhs_load(u):
        slot = lax.rem(u, 2)
        return pltpu.make_async_copy(rhs_ref.at[rows(u)], rb_ref.at[slot], rload.at[slot])

    def store(u):
        slot = lax.rem(u, 2)
        return pltpu.make_async_copy(rb_ref.at[slot], out_ref.at[rows(u)], rstore.at[slot])

    def update(u):
        slot = lax.rem(u, 2)

        @pl.loop(0, PANELS)
        def _(p):
            at = pl.ds(pl.multiple_of(p * PANEL, PANEL), PANEL)
            tile = full_ref[u - 1, p].reshape(PANEL, wide).T
            ah_ref[:wide, at], al_ref[:wide, at] = split(tile)

        rhs_load(u).wait()

        @pl.when(u > 1)
        def _():
            store(u - 1).wait()

        @pl.when(u + 1 < tiles)
        def _():
            rhs_load(u + 1).start()

        @pl.loop(0, columns // part)
        def _(n):
            at = chunk(n)
            total = product(
                ah_ref[:window, :], al_ref[:window, :], high_ref[:, at], low_ref[:, at]
            )
            rb_ref[slot, :, at] = rb_ref[slot, :, at] - total

        store(u).start()

    def tail_store(j):
        at = pl.multiple_of(j * thin, thin)
        return pltpu.make_async_copy(
            rb_ref.at[last % 2, pl.ds(at, thin)],
            out_ref.at[pl.ds(pl.multiple_of(last * window + at, thin), thin)],
            tail_done.at[j],
        )

    def tail_update(j):
        @pl.loop(0, PANELS)
        def _(p):
            at = pl.ds(pl.multiple_of(p * PANEL, PANEL), PANEL)
            tile = tail_ref[j, p].reshape(PANEL, slim).T
            ah_ref[:slim, at], al_ref[:slim, at] = split(tile)

        total = product(ah_ref[:thin, :], al_ref[:thin, :], high_ref[...], low_ref[...])
        at = pl.ds(pl.multiple_of(j * thin, thin), thin)
        rb_ref[last % 2, at, :] = rb_ref[last % 2, at, :] - total
        tail_store(j).start()

    def keep(t):
        first = isinstance(t, int)
        here = lt_ref.at[row, :, col] if first else buffer(col, t)
        return pltpu.make_async_copy(own_ref.at[:, :, lanes(t)], here, stay_sem.at[t])

    x_stay = pltpu.make_async_copy(rhs_ref.at[pl.ds(0, window)], x_ref.at[row], xstay)

    lead = min(3, last)
    ahead = min(5, last)
    first_launch()
    keep(0).start()

    @pl.loop(1, last)
    def _(t):
        keep(t).start()

    @pl.loop(0, subs)
    def _(j):
        tail_keep(j).start()

    share(x_copy)
    x_stay.start()
    pl.loop(1, lead)(launch)
    for ring in rings:
        first_pass(ring)
    keep(0).wait()

    @pl.loop(1, last)
    def _(t):
        keep(t).wait()

    @pl.loop(0, subs)
    def _(j):
        tail_keep(j).wait()

    for make in l_copies:
        share(make)
    pl.loop(lead, ahead)(launch)
    rhs_load(1).start()
    invert_own()
    for m in range(1, peers):
        i_copy(row, m).start()
    share_on(x_copy)

    begin = 0
    catch = begin + PANELS
    rate = -(-(last - 1) // (last - catch))
    lags = [len(rings) - 1 - d for d in range(len(rings))]
    start = 1 - max(lags)

    solved = pltpu.make_async_copy(x_ref.at[row], out_ref.at[pl.ds(0, window)], ostore)

    @pl.loop(start, last)
    def _(s):
        @pl.when(s + ahead - start < last)
        def _():
            launch(s + ahead - start)

        @pl.when(s + ahead - start == last)
        def _():
            pl.loop(0, subs)(tail_launch)

        for lag, ring in zip(lags, rings):
            t = s + lag

            @pl.when((t >= 1) & (t < last))
            def _(t=t, ring=ring):
                pass_on(t, ring)

            @pl.when(t == last)
            def _(ring=ring):
                pl.loop(0, subs)(functools.partial(tail_pass, ring=ring))

        @pl.when(s == begin)
        def _():
            for make in l_copies:
                share_on(make)
            share_end(x_copy)
            x_stay.wait()
            for make in l_copies:
                share_end(make)
            for m in range(1, peers):
                i_copy(row, m).wait_send()
                i_copy(lax.rem(row + peers - m, peers), m).wait_recv()

        for p in range(PANELS):

            @pl.when(s == begin + p)
            def _(p=p):
                solve(p)

        @pl.when(s == catch - 1)
        def _():
            solved.start()

        @pl.when(s >= catch)
        def _():
            low = jnp.minimum(rate * (s - catch) + 1, s)
            high = jnp.minimum(rate * (s - catch) + rate, s)

            @pl.loop(low, high + 1)
            def _(u):
                update(u)

    rhs_load(last).wait()

    @pl.loop(0, subs)
    def _(j):
        tail_pass(j, rings[-1])
        tail_update(j)

    first_end()
    pl.loop(0, subs)(tail_end)

    @pl.loop(1, last)
    def _(t):
        for side, use in targets(0, 0, t):

            @pl.when(use)
            def _(side=side):
                copy(own_ref.at[:, :, lanes(t)], col, t, side).wait_send()

        for da, db in offsets:

            @pl.when(inside(da, db))
            def _(da=da, db=db):
                block = place(da, db)
                for side, use in targets(da, db, t):

                    @pl.when(use)
                    def _(side=side):
                        copy(own_ref.at[:, :, lanes(t)], block, t, side).wait_send()

    store(last - 1).wait()

    @pl.loop(0, subs)
    def _(j):
        tail_store(j).wait()

    solved.wait()


def whiten(rhs, own, outer, inner, peers):
    blocks = outer * inner
    window = PANELS * (PANEL // peers)
    tiles = rhs.shape[0] // window
    wide = own.shape[-1] // tiles
    subs = window // 128 if window % 128 == 0 else 1
    piece = PANEL // blocks
    rp = PANEL // peers
    columns = rhs.shape[1]
    total = PANELS * PANEL
    half = peers // 2
    deepest = max(wide, PANEL)
    dma = pltpu.SemaphoreType.DMA
    any_space = pl.BlockSpec(memory_space=pl.ANY)
    return pl.pallas_call(
        functools.partial(kernel, outer, inner, peers),
        out_shape=jax.ShapeDtypeStruct(rhs.shape, rhs.dtype),
        in_specs=[any_space] * 2,
        out_specs=any_space,
        scratch_shapes=[
            pltpu.VMEM((tiles - 2, PANELS, blocks, piece, wide), jnp.float32),
            pltpu.VMEM((subs, PANELS, blocks, piece, wide // subs), jnp.float32),
            pltpu.VMEM((peers, window, columns), jnp.float32),
            pltpu.VMEM((peers, PANELS, blocks, piece, wide), jnp.float32),
            pltpu.VMEM((peers, PANELS, rp, rp), jnp.float32),
            pltpu.VMEM((total, columns), BF16),
            pltpu.VMEM((total, columns), BF16),
            pltpu.VMEM((2, window, columns), jnp.float32),
            pltpu.VMEM((deepest, total), BF16),
            pltpu.VMEM((deepest, total), BF16),
            dma((4, blocks, PANELS)),
            dma((blocks, PANELS)),
            dma((4, blocks, tiles)),
            dma((blocks, tiles)),
            dma((tiles,)),
            dma((2 * half,)),
            dma((peers,)),
            dma,
            dma((2 * half, PANELS)),
            dma((peers, PANELS)),
            dma((peers,)),
            dma((peers,)),
            dma((2,)),
            dma((2,)),
            dma,
            dma((4, blocks, subs)),
            dma((blocks, subs)),
            dma((subs,)),
            dma((subs,)),
        ],
        compiler_params=pltpu.CompilerParams(
            collective_id=0, has_side_effects=True, vmem_limit_bytes=67_043_328
        ),
        cost_estimate=pl.CostEstimate(
            flops=6 * rhs.shape[0] * total * columns,
            bytes_accessed=16 * rhs.size,
            transcendentals=0,
        ),
    )(rhs, own)


def local(rhs_tile, factor, inner):
    peers = lax.axis_size("row")
    blocks = lax.axis_size("col")
    window = PANELS * (PANEL // peers)
    own = factor.T.reshape(PANELS, PANEL // blocks, factor.shape[0])
    if window % 128:
        own = own.reshape(PANELS, PANEL // blocks, -1, window)
        own = jnp.pad(own, ((0, 0), (0, 0), (0, 0), (0, -window % 128)))
        own = own.reshape(PANELS, PANEL // blocks, -1)
    return whiten(rhs_tile, own, blocks // inner, inner, peers)


def inner_size(mesh):
    count = mesh.shape["col"]
    try:
        where = [tuple(d.coords) for d in mesh.devices.reshape(-1, count)[0]]
        inner = 1
        while inner < count and sum(p != q for p, q in zip(where[inner], where[0])) == 1 and (
            inner == 1 or [p != q for p, q in zip(where[inner], where[0])]
            == [p != q for p, q in zip(where[1], where[0])]
        ):
            inner += 1
        if count % inner == 0:
            return inner
    except Exception:
        pass
    return 2 if count % 2 == 0 else 1


def solution(mesh):
    specs = P("row", "col")
    body = functools.partial(local, inner=inner_size(mesh))
    return jax.shard_map(body, mesh=mesh, in_specs=(specs, specs), out_specs=specs, check_vma=False)
```
